32 devices in a mesh: gx: 8 (over z, core), gz: 4 (over y, x).
Axes of the slice: x: 2, y: 2, z: 4, core: 2. Of those that a mesh axis runs over, the one named last changes fastest.
Arguments:
- fields: bfloat16 [4, 4, 512, 8192], P(None, None, 'gz', 'gx'), may hold values from -6 to 6
- strat_sq: float32 [512], P('gz'), may hold values from 0.3 to 3
Outputs:
- tendency: float32 [4, 4, 512, 8192], P(None, None, 'gz', 'gx')
The draws below stay inside these ranges and needn't reach their ends.
All inputs are finite; a program needn't handle non-finite values.
Results may differ from the reference program's by a relative error of at most 0.0003.
Values may be sent and summed in bfloat16 or wider, within the bound.
No kernel may reach another device: no remote copies, remote signals or barrier semaphores. Data moves between devices by JAX's collectives and lax.ppermute only.
A program may use at most 128 MiB of HBM per device.

```python
import math
import jax
import jax.numpy as jnp
from jax import lax

NX = 8192
LINES = 4
NZ = 512


def block_levels(rng, extent, cuts, least, high):
    level = 1.0
    for dim, shards_of in cuts:
        steps = jax.random.uniform(jax.random.fold_in(jax.random.fold_in(rng, 6), dim), (shards_of,), jnp.float32, least / len(cuts), high / len(cuts))
        level = level * jnp.repeat(jnp.exp(steps), extent[dim] // shards_of).reshape((-1,) + (1,) * (len(extent) - 1 - dim))
    return level


def bell_draw(stream_key, dims, scale, bound, pieces=(), kind=jnp.bfloat16):
    array = scale * jax.random.normal(stream_key, dims, jnp.float32)
    if pieces:
        array = array * block_levels(stream_key, dims, pieces, -0.22, 0.18)
    return jnp.clip(array, -bound, bound).astype(kind)


def setup_inputs(seed: int = 0) -> dict:
    keys = jax.random.split(jax.random.key(seed), 3)
    return {
        "fields": bell_draw(keys[0], (4, LINES, NZ, NX), 1.0, 6.0, ((2, 4), (3, 8))),
        "strat_sq": jnp.clip(jnp.exp(math.log(3.0) - 2.3025851 * jax.random.uniform(keys[1], (NZ,), jnp.float32) ** block_levels(keys[1], (NZ,), ((0, 4),), -0.2, 0.2)), 0.3, 3.0),
    }


TWO_PI = 2.0 * math.pi
STENCIL = (4.0 / 5.0, -1.0 / 5.0, 4.0 / 105.0, -1.0 / 280.0)


def vertical(padded, levels):
    result = jnp.zeros_like(padded[:, :, 4:4 + levels])
    for offset in range(1, 5):
        weight = STENCIL[offset - 1]
        result = result + weight * (padded[:, :, 4 + offset:4 + offset + levels] - padded[:, :, 4 - offset:4 - offset + levels])
    return result


def tendencies(values, slope_x, slope_z, strat_col):
    speed_u = values[0]
    speed_w = values[2]
    advect = -(speed_u[None] * slope_x + speed_w[None] * slope_z)
    return jnp.stack([advect[0], advect[1], advect[2] + values[3], advect[3] - strat_col * speed_w])


def reference(fields, strat_sq):
    values = fields.astype(jnp.float32)
    index_all = jnp.arange(NX)
    wavenum = jnp.where(index_all < NX // 2, index_all, index_all - NX).astype(values.dtype) * (TWO_PI / NX)
    wavenum = jnp.where(index_all == NX // 2, jnp.zeros_like(wavenum), wavenum)

    def derive(series):
        spectrum = jnp.fft.fft(series, axis=-1)
        return jnp.real(jnp.fft.ifft(1j * wavenum * spectrum, axis=-1)).astype(series.dtype)

    slope_x = lax.map(derive, values)
    padded = jnp.pad(values, ((0, 0), (0, 0), (4, 4), (0, 0)))
    slope_z = vertical(padded, NZ)
    return tendencies(values, slope_x, slope_z, strat_sq[:, None])
```

```python
import functools
import math

import jax
import jax.numpy as jnp
import numpy as np
from jax import lax
from jax.experimental import pallas as pl
from jax.experimental.pallas import tpu as pltpu
from jax.sharding import PartitionSpec as P

STENCIL = (4.0 / 5.0, -1.0 / 5.0, 4.0 / 105.0, -1.0 / 280.0)
BAND = 256
CHUNKS = 2
F32 = jnp.float32
BF16 = jnp.bfloat16


def kernel_row(length):
    index = np.arange(length)
    signed = np.where(index < length // 2, index, index - length).astype(np.float64)
    angle = np.pi * np.where(signed == 0, 1.0, signed) / length
    row = np.where(index % 2 == 0, 1.0, -1.0) * (np.pi / length) / np.tan(angle)
    row = np.where((index == 0) | (index == length // 2), 0.0, row)
    return jnp.asarray(row.astype(np.float32))[None, :]


def strip_body(pad, row_ref, high_ref, low_ref, run_ref):
    rows, length = run_ref.shape

    @pl.when(pl.program_id(0) == 0)
    def _():
        wide = jnp.broadcast_to(row_ref[...], (rows, length))
        run_ref[...] = pltpu.roll(wide, pad, 1, stride=1, stride_axis=0)

    @pl.when(pl.program_id(0) > 0)
    def _():
        run_ref[...] = pltpu.roll(run_ref[...], rows, 1)

    run = run_ref[...]
    high = run.astype(BF16)
    low = (run - high.astype(F32)).astype(BF16)
    high_ref[:, :length] = high
    low_ref[:, :length] = low
    if pad:
        high_ref[:, length:] = high[:, :pad]
        low_ref[:, length:] = low[:, :pad]


def strips(length, width):
    pad = width - BAND
    rows = 16
    shape = jax.ShapeDtypeStruct((BAND, length + pad), BF16)
    spec = pl.BlockSpec((rows, length + pad), lambda i: (i, 0))
    return pl.pallas_call(
        functools.partial(strip_body, pad),
        grid=(BAND // rows,),
        in_specs=[pl.BlockSpec((1, length), lambda i: (0, 0))],
        out_specs=[spec, spec],
        out_shape=[shape, shape],
        scratch_shapes=[pltpu.VMEM((rows, length), F32)],
        cost_estimate=pl.CostEstimate(
            flops=4 * BAND * length, bytes_accessed=4 * BAND * length, transcendentals=0
        ),
    )(kernel_row(length))


def panel(strip_ref, first, width, columns):
    runs = [
        strip_ref[:, pl.ds(pl.multiple_of(first + width - BAND - BAND * i, BAND), columns)]
        for i in range(width // BAND)
    ]
    return runs[0] if len(runs) == 1 else jnp.concatenate(runs, axis=0)


def dot(left, right):
    return jnp.dot(left, right, preferred_element_type=F32)


def far_body(devices, lines_ref, high_ref, low_ref, out_ref):
    total_rows, width = lines_ref.shape
    rows = total_rows // devices
    columns = out_ref.shape[1]
    column = pl.program_id(0) * columns
    total = None
    for step in range(1, devices):
        cut = (devices - step) * rows
        moved = jnp.concatenate([lines_ref[cut:, :], lines_ref[:cut, :]], axis=0)
        first = step * width + column
        for strip_ref in (high_ref, low_ref):
            part = dot(moved, panel(strip_ref, first, width, columns))
            total = part if total is None else total + part
    out_ref[...] = total.astype(BF16)


def far_slopes(lines, high, low):
    devices, rows, width = lines.shape
    total_rows = devices * rows
    columns = BAND
    out = pl.pallas_call(
        functools.partial(far_body, devices),
        grid=(width // columns,),
        in_specs=[
            pl.BlockSpec((total_rows, width), lambda j: (0, 0)),
            pl.BlockSpec(high.shape, lambda j: (0, 0)),
            pl.BlockSpec(low.shape, lambda j: (0, 0)),
        ],
        out_specs=pl.BlockSpec((total_rows, columns), lambda j: (0, j)),
        out_shape=jax.ShapeDtypeStruct((total_rows, width), BF16),
        compiler_params=pltpu.CompilerParams(vmem_limit_bytes=48 * 2**20),
        cost_estimate=pl.CostEstimate(
            flops=4 * total_rows * (devices - 1) * width * width,
            bytes_accessed=4 * total_rows * width + 4 * high.size,
            transcendentals=0,
        ),
    )(lines.reshape(total_rows, width), high, low)
    return out.reshape(devices, rows, width)


def local_body(field_ref, u_ref, w_ref, b_ref, below_ref, above_ref, strat_ref, high_ref, low_ref, out_ref, pad_ref):
    comp = pl.program_id(1)
    levels, width = out_ref.shape
    pad_ref[8 : 8 + levels, :] = field_ref[...].astype(F32)
    pad_ref[4:8, :] = below_ref[...].astype(F32)
    pad_ref[8 + levels : 12 + levels, :] = above_ref[...].astype(F32)
    is_w = (comp == 2).astype(F32)
    is_b = (comp == 3).astype(F32)
    strat = strat_ref[...] * is_b
    columns = BAND
    for j in range(width // columns):
        here = slice(j * columns, (j + 1) * columns)
        near = dot(field_ref[...], panel(high_ref, j * columns, width, columns)) + dot(
            field_ref[...], panel(low_ref, j * columns, width, columns)
        )
        slope_z = None
        for offset in range(1, 5):
            term = STENCIL[offset - 1] * (
                pad_ref[8 + offset : 8 + offset + levels, here]
                - pad_ref[8 - offset : 8 - offset + levels, here]
            )
            slope_z = term if slope_z is None else slope_z + term
        speed_w = w_ref[:, here].astype(F32)
        out_ref[:, here] = (
            is_w * b_ref[:, here].astype(F32)
            - strat * speed_w
            - (u_ref[:, here].astype(F32) * near + speed_w * slope_z)
        )


def local_part(fields, below, above, strat_col, high, low):
    comps, lines, levels, width = fields.shape

    def block(comp):
        return pl.BlockSpec(
            (None, None, levels, width),
            (lambda l, c: (c, l, 0, 0)) if comp is None else (lambda l, c: (comp, l, 0, 0)),
        )

    halo = pl.BlockSpec((None, None, 4, width), lambda l, c: (c, l, 0, 0))
    whole = pl.BlockSpec(high.shape, lambda l, c: (0, 0))
    return pl.pallas_call(
        local_body,
        grid=(lines, comps),
        in_specs=[
            block(None),
            block(0),
            block(2),
            block(3),
            halo,
            halo,
            pl.BlockSpec((levels, 1), lambda l, c: (0, 0)),
            whole,
            whole,
        ],
        out_specs=block(None),
        out_shape=jax.ShapeDtypeStruct(fields.shape, F32),
        scratch_shapes=[pltpu.VMEM((levels + 16, width), F32)],
        compiler_params=pltpu.CompilerParams(vmem_limit_bytes=56 * 2**20),
        cost_estimate=pl.CostEstimate(
            flops=4 * fields.size * width, bytes_accessed=8 * fields.size, transcendentals=0
        ),
    )(fields, fields, fields, fields, below, above, strat_col, high, low)


def update_body(part_ref, u_ref, far_ref, out_ref):
    out_ref[...] = part_ref[...] - u_ref[...].astype(F32) * far_ref[...].astype(F32)


def update(part, fields, far, comp):
    comps, lines, levels, width = fields.shape
    spec = pl.BlockSpec((None, None, levels, width), lambda l, c: (comp + c, l, 0, 0))
    return pl.pallas_call(
        update_body,
        grid=(lines, far.shape[0]),
        in_specs=[
            spec,
            pl.BlockSpec((None, None, levels, width), lambda l, c: (0, l, 0, 0)),
            pl.BlockSpec((None, None, levels, width), lambda l, c: (c, l, 0, 0)),
        ],
        out_specs=spec,
        out_shape=jax.ShapeDtypeStruct(part.shape, F32),
        input_output_aliases={0: 0},
        cost_estimate=pl.CostEstimate(
            flops=2 * far.size, bytes_accessed=12 * far.size, transcendentals=0
        ),
    )(part, fields, far)


def halos(fields):
    count = lax.axis_size("gz")
    forward = [(i, i + 1) for i in range(count - 1)]
    backward = [(target, source) for source, target in forward]
    levels = fields.shape[2]
    below = lax.ppermute(fields[:, :, levels - 4 :], "gz", forward)
    above = lax.ppermute(fields[:, :, :4], "gz", backward)
    return below, above


def body(fields, strat_sq):
    comps, lines, levels, width = fields.shape
    devices = lax.axis_size("gx")
    group = comps // CHUNKS
    shape = (devices, group * lines * levels // devices, width)
    gathered = [
        lax.all_to_all(
            fields[c : c + group].reshape(shape), "gx", split_axis=0, concat_axis=0, tiled=True
        )
        for c in range(0, comps, group)
    ]
    below, above = halos(fields)
    high, low = strips(devices * width, width)
    part = local_part(fields, below, above, strat_sq[:, None], high, low)
    for i in range(CHUNKS):
        far = far_slopes(gathered[i], high, low)
        back = lax.all_to_all(far, "gx", split_axis=0, concat_axis=0, tiled=True)
        part = update(part, fields, back.reshape(group, lines, levels, width), i * group)
    return part


def solution(mesh):
    placed = (P(None, None, "gz", "gx"), P("gz"))
    return jax.shard_map(
        body, mesh=mesh, in_specs=placed, out_specs=P(None, None, "gz", "gx"), check_vma=False
    )
```

```python
import functools
import math

import jax
import jax.numpy as jnp
import numpy as np
from jax import lax
from jax.experimental import pallas as pl
from jax.experimental.pallas import tpu as pltpu
from jax.sharding import PartitionSpec as P

STENCIL = (4.0 / 5.0, -1.0 / 5.0, 4.0 / 105.0, -1.0 / 280.0)
BAND = 256
UPDATE_CUTS = (4, 6)
UPDATE_VMEM = 60 * 2**20
F32 = jnp.float32
BF16 = jnp.bfloat16


def kernel_row(length):
    index = np.arange(length)
    signed = np.where(index < length // 2, index, index - length).astype(np.float64)
    angle = np.pi * np.where(signed == 0, 1.0, signed) / length
    row = np.where(index % 2 == 0, 1.0, -1.0) * (np.pi / length) / np.tan(angle)
    row = np.where((index == 0) | (index == length // 2), 0.0, row)
    return jnp.asarray(row.astype(np.float32))[None, :]


def strip_body(pad, row_ref, high_ref, low_ref, run_ref):
    rows, length = run_ref.shape

    @pl.when(pl.program_id(0) == 0)
    def _():
        wide = jnp.broadcast_to(row_ref[...], (rows, length))
        run_ref[...] = pltpu.roll(wide, pad, 1, stride=1, stride_axis=0)

    @pl.when(pl.program_id(0) > 0)
    def _():
        run_ref[...] = pltpu.roll(run_ref[...], rows, 1)

    run = run_ref[...]
    high = run.astype(BF16)
    low = (run - high.astype(F32)).astype(BF16)
    high_ref[:, :length] = high
    low_ref[:, :length] = low
    if pad:
        high_ref[:, length:] = high[:, :pad]
        low_ref[:, length:] = low[:, :pad]


def strips(length, width):
    pad = width - BAND
    rows = 16
    shape = jax.ShapeDtypeStruct((BAND, length + pad), BF16)
    spec = pl.BlockSpec((rows, length + pad), lambda i: (i, 0))
    return pl.pallas_call(
        functools.partial(strip_body, pad),
        grid=(BAND // rows,),
        in_specs=[pl.BlockSpec((1, length), lambda i: (0, 0))],
        out_specs=[spec, spec],
        out_shape=[shape, shape],
        scratch_shapes=[pltpu.VMEM((rows, length), F32)],
        cost_estimate=pl.CostEstimate(
            flops=4 * BAND * length, bytes_accessed=4 * BAND * length, transcendentals=0
        ),
    )(kernel_row(length))


def panel(strip_ref, first, width, columns):
    runs = [
        strip_ref[:, pl.ds(pl.multiple_of(first + width - BAND - BAND * i, BAND), columns)]
        for i in range(width // BAND)
    ]
    return runs[0] if len(runs) == 1 else jnp.concatenate(runs, axis=0)


def dot(left, right):
    return jnp.dot(left, right, preferred_element_type=F32)


def far_sum(devices, column, columns, lines_ref, high_ref, low_ref):
    total_rows, width = lines_ref.shape
    rows = total_rows // devices
    total = None
    for step in range(1, devices):
        cut = (devices - step) * rows
        moved = jnp.concatenate([lines_ref[cut:, :], lines_ref[:cut, :]], axis=0)
        first = step * width + column
        for strip_ref in (high_ref, low_ref):
            part = dot(moved, panel(strip_ref, first, width, columns))
            total = part if total is None else total + part
    return total.astype(BF16)


def far_body(devices, me_ref, lines_ref, high_ref, low_ref, out_ref):
    columns = out_ref.shape[1]
    out_ref[...] = far_sum(
        devices, pl.program_id(0) * columns, columns, lines_ref, high_ref, low_ref
    )


def far_blocks_body(devices, me_ref, lines_ref, high_ref, low_ref, *refs):
    outs, all_ref = refs[:-1], refs[-1]
    rows, columns = outs[0].shape
    all_ref[...] = far_sum(
        devices, pl.program_id(0) * columns, columns, lines_ref, high_ref, low_ref
    )
    for k in range(devices):
        start = pl.multiple_of((me_ref[0] + devices - k) % devices * rows, rows)
        outs[k][...] = all_ref[pl.ds(start, rows), :]


def far_slopes(lines, high, low, me, split):
    devices, rows, width = lines.shape
    total_rows = devices * rows
    columns = BAND
    whole = pl.BlockSpec((total_rows, width), lambda j, m: (0, 0))
    strip = pl.BlockSpec(high.shape, lambda j, m: (0, 0), pipeline_mode=pl.Buffered(1))
    held, count = (rows, devices) if split else (total_rows, 1)
    out = pl.pallas_call(
        functools.partial(far_blocks_body if split else far_body, devices),
        grid_spec=pltpu.PrefetchScalarGridSpec(
            num_scalar_prefetch=1,
            grid=(width // columns,),
            in_specs=[whole, strip, strip],
            out_specs=[pl.BlockSpec((held, columns), lambda j, m: (0, j))] * count,
            scratch_shapes=[pltpu.VMEM((total_rows, columns), BF16)] if split else [],
        ),
        out_shape=[jax.ShapeDtypeStruct((held, width), BF16)] * count,
        compiler_params=pltpu.CompilerParams(vmem_limit_bytes=28 * 2**20),
        cost_estimate=pl.CostEstimate(
            flops=4 * total_rows * (devices - 1) * width * width,
            bytes_accessed=4 * total_rows * width + 4 * high.size,
            transcendentals=0,
        ),
    )(me, lines.reshape(total_rows, width), high, low)
    return out if split else out[0].reshape(devices, rows, width)


def local_body(field_ref, u_ref, w_ref, b_ref, below_ref, above_ref, strat_ref, high_ref, low_ref, out_ref, pad_ref):
    comp = pl.program_id(1)
    levels, width = out_ref.shape
    pad_ref[8 : 8 + levels, :] = field_ref[...].astype(F32)
    pad_ref[4:8, :] = below_ref[...].astype(F32)
    pad_ref[8 + levels : 12 + levels, :] = above_ref[...].astype(F32)
    is_w = (comp == 2).astype(F32)
    is_b = (comp == 3).astype(F32)
    strat = strat_ref[...] * is_b
    columns = BAND
    for j in range(width // columns):
        here = slice(j * columns, (j + 1) * columns)
        near = dot(field_ref[...], panel(high_ref, j * columns, width, columns)) + dot(
            field_ref[...], panel(low_ref, j * columns, width, columns)
        )
        slope_z = None
        for offset in range(1, 5):
            term = STENCIL[offset - 1] * (
                pad_ref[8 + offset : 8 + offset + levels, here]
                - pad_ref[8 - offset : 8 - offset + levels, here]
            )
            slope_z = term if slope_z is None else slope_z + term
        speed_w = w_ref[:, here].astype(F32)
        out_ref[:, here] = (
            is_w * b_ref[:, here].astype(F32)
            - strat * speed_w
            - (u_ref[:, here].astype(F32) * near + speed_w * slope_z)
        )


def local_part(fields, below, above, strat_col, high, low):
    comps, lines, levels, width = fields.shape

    def block(comp):
        return pl.BlockSpec(
            (None, None, levels, width),
            (lambda l, c: (c, l, 0, 0)) if comp is None else (lambda l, c: (comp, l, 0, 0)),
        )

    halo = pl.BlockSpec((None, None, 4, width), lambda l, c: (c, l, 0, 0))
    whole = pl.BlockSpec(high.shape, lambda l, c: (0, 0), pipeline_mode=pl.Buffered(1))
    return pl.pallas_call(
        local_body,
        grid=(lines, comps),
        in_specs=[
            block(None),
            block(0),
            block(2),
            block(3),
            halo,
            halo,
            pl.BlockSpec((levels, 1), lambda l, c: (0, 0)),
            whole,
            whole,
        ],
        out_specs=block(None),
        out_shape=jax.ShapeDtypeStruct(fields.shape, F32),
        scratch_shapes=[pltpu.VMEM((levels + 16, width), F32)],
        compiler_params=pltpu.CompilerParams(vmem_limit_bytes=28 * 2**20),
        cost_estimate=pl.CostEstimate(
            flops=4 * fields.size * width, bytes_accessed=8 * fields.size, transcendentals=0
        ),
    )(fields, fields, fields, fields, below, above, strat_col, high, low)


def update_body(part_ref, u_ref, far_ref, out_ref):
    out_ref[...] = part_ref[...] - u_ref[...].astype(F32) * far_ref[...].astype(F32)


def update(part, fields, far, comp):
    comps, lines, levels, width = fields.shape
    spec = pl.BlockSpec((None, None, levels, width), lambda l, c: (comp + c, l, 0, 0))
    return pl.pallas_call(
        update_body,
        grid=(lines, far.shape[0]),
        in_specs=[
            spec,
            pl.BlockSpec((None, None, levels, width), lambda l, c: (0, l, 0, 0)),
            pl.BlockSpec((None, None, levels, width), lambda l, c: (c, l, 0, 0)),
        ],
        out_specs=spec,
        out_shape=jax.ShapeDtypeStruct(part.shape, F32),
        input_output_aliases={0: 0},
        compiler_params=pltpu.CompilerParams(vmem_limit_bytes=UPDATE_VMEM),
        cost_estimate=pl.CostEstimate(
            flops=2 * far.size, bytes_accessed=12 * far.size, transcendentals=0
        ),
    )(part, fields, far)


def update_blocks_body(offsets, me_ref, part_ref, u_ref, *refs):
    fars, out_ref = refs[:-1], refs[-1]
    for i, far_ref in enumerate(fars):

        @pl.when(pl.program_id(0) == i)
        def _(far_ref=far_ref):
            out_ref[...] = part_ref[...] - u_ref[...].astype(F32) * far_ref[...].astype(F32)


def update_blocks(part, fields, base, offsets, fars, me, devices, lines_levels):
    rows, width = fars[0].shape
    u_blocks = lines_levels // rows

    def owner(i, m):
        offset = offsets[-1]
        for index in range(len(offsets) - 1):
            offset = jnp.where(i == index, offsets[index], offset)
        return (m[0] + offset) % devices

    spec = pl.BlockSpec((rows, width), lambda i, m: (base + owner(i, m), 0))
    return pl.pallas_call(
        functools.partial(update_blocks_body, offsets),
        grid_spec=pltpu.PrefetchScalarGridSpec(
            num_scalar_prefetch=1,
            grid=(len(offsets),),
            in_specs=[spec, pl.BlockSpec((rows, width), lambda i, m: (owner(i, m) % u_blocks, 0))]
            + [pl.BlockSpec((rows, width), lambda i, m: (0, 0))] * len(offsets),
            out_specs=spec,
        ),
        out_shape=jax.ShapeDtypeStruct(part.shape, F32),
        input_output_aliases={1: 0},
        compiler_params=pltpu.CompilerParams(vmem_limit_bytes=UPDATE_VMEM),
        cost_estimate=pl.CostEstimate(
            flops=2 * len(offsets) * rows * width,
            bytes_accessed=12 * len(offsets) * rows * width,
            transcendentals=0,
        ),
    )(me, part, fields, *fars)


def order_of(devices):
    return sorted(range(1, devices), key=lambda k: abs(2 * k - devices))


def groups_of(devices, cuts):
    order = [0] + order_of(devices)
    marks = [0] + [devices * cut // 8 for cut in cuts] + [devices]
    return [order[a:b] for a, b in zip(marks, marks[1:])]


def halos(fields):
    count = lax.axis_size("gz")
    forward = [(i, i + 1) for i in range(count - 1)]
    backward = [(target, source) for source, target in forward]
    levels = fields.shape[2]
    below = lax.ppermute(fields[:, :, levels - 4 :], "gz", forward)
    above = lax.ppermute(fields[:, :, :4], "gz", backward)
    return below, above


def body(fields, strat_sq):
    comps, lines, levels, width = fields.shape
    devices = lax.axis_size("gx")
    group = comps // 2
    shape = (devices, group * lines * levels // devices, width)
    me = lax.axis_index("gx").astype(jnp.int32)[None]

    def exchange(whole):
        return lax.all_to_all(whole, "gx", split_axis=0, concat_axis=0, tiled=True)

    def ahead(block, k):
        return lax.ppermute(block, "gx", [(i, (i + k) % devices) for i in range(devices)])

    first = exchange(fields[:group].reshape(shape))
    below, above = halos(fields)
    high, low = strips(devices * width, width)
    part = local_part(fields, below, above, strat_sq[:, None], high, low)
    source, part = lax.optimization_barrier((fields, part))
    second = exchange(source[group:].reshape(shape))
    back = exchange(far_slopes(first, high, low, me, False))
    outs = far_slopes(second, high, low, me, True)
    fars = {0: outs[0]}
    for k in order_of(devices):
        fars[k] = ahead(outs[k], devices - k)
    part = update(part, fields, back.reshape(group, lines, levels, width), 0)
    flat = fields.reshape(comps * lines * levels, width)
    part = part.reshape(flat.shape)
    for offsets in groups_of(devices, UPDATE_CUTS):
        part = update_blocks(
            part, flat, devices, offsets, [fars[k] for k in offsets], me, devices, lines * levels
        )
    return part.reshape(fields.shape)


def solution(mesh):
    placed = (P(None, None, "gz", "gx"), P("gz"))
    return jax.shard_map(
        body, mesh=mesh, in_specs=placed, out_specs=P(None, None, "gz", "gx"), check_vma=False
    )
```

```python
import functools
import math

import jax
import jax.numpy as jnp
import numpy as np
from jax import lax
from jax.experimental import pallas as pl
from jax.experimental.pallas import tpu as pltpu
from jax.sharding import PartitionSpec as P

STENCIL = (4.0 / 5.0, -1.0 / 5.0, 4.0 / 105.0, -1.0 / 280.0)
BAND = 128
COLUMNS = 256
UPDATE_VMEM = 16 * 2**20
F32 = jnp.float32
BF16 = jnp.bfloat16


def kernel_row(length):
    index = np.arange(length)
    signed = np.where(index < length // 2, index, index - length).astype(np.float64)
    angle = np.pi * np.where(signed == 0, 1.0, signed) / length
    row = np.where(index % 2 == 0, 1.0, -1.0) * (np.pi / length) / np.tan(angle)
    row = np.where((index == 0) | (index == length // 2), 0.0, row)
    return jnp.asarray(row.astype(np.float32))[None, :]


def strip_body(pad, row_ref, high_ref, low_ref, run_ref):
    rows, length = run_ref.shape

    @pl.when(pl.program_id(0) == 0)
    def _():
        wide = jnp.broadcast_to(row_ref[...], (rows, length))
        run_ref[...] = pltpu.roll(wide, pad, 1, stride=1, stride_axis=0)

    @pl.when(pl.program_id(0) > 0)
    def _():
        run_ref[...] = pltpu.roll(run_ref[...], rows, 1)

    run = run_ref[...]
    high = run.astype(BF16)
    low = (run - high.astype(F32)).astype(BF16)
    high_ref[:, :length] = high
    low_ref[:, :length] = low
    if pad:
        high_ref[:, length:] = high[:, :pad]
        low_ref[:, length:] = low[:, :pad]


def strips(length, width):
    pad = width - BAND
    rows = 16
    shape = jax.ShapeDtypeStruct((BAND, length + pad), BF16)
    spec = pl.BlockSpec((rows, length + pad), lambda i: (i, 0))
    return pl.pallas_call(
        functools.partial(strip_body, pad),
        grid=(BAND // rows,),
        in_specs=[pl.BlockSpec((1, length), lambda i: (0, 0))],
        out_specs=[spec, spec],
        out_shape=[shape, shape],
        scratch_shapes=[pltpu.VMEM((rows, length), F32)],
        compiler_params=pltpu.CompilerParams(vmem_limit_bytes=8 * 2**20),
        cost_estimate=pl.CostEstimate(
            flops=4 * BAND * length, bytes_accessed=4 * BAND * length, transcendentals=0
        ),
    )(kernel_row(length))


def panel(strip_ref, first, width, columns):
    runs = [
        strip_ref[:, pl.ds(pl.multiple_of(first + width - BAND - BAND * i, BAND), columns)]
        for i in range(width // BAND)
    ]
    return runs[0] if len(runs) == 1 else jnp.concatenate(runs, axis=0)


def dot(left, right):
    return jnp.dot(left, right, preferred_element_type=F32)


def far_sum(devices, column, columns, lines_ref, high_ref, low_ref):
    total_rows, width = lines_ref.shape
    rows = total_rows // devices
    total = None
    for step in range(1, devices):
        cut = (devices - step) * rows
        moved = jnp.concatenate([lines_ref[cut:, :], lines_ref[:cut, :]], axis=0)
        first = step * width + column
        for strip_ref in (high_ref, low_ref):
            part = dot(moved, panel(strip_ref, first, width, columns))
            total = part if total is None else total + part
    return total.astype(BF16)


def far_blocks_body(devices, me_ref, lines_ref, high_ref, low_ref, *refs):
    outs, all_ref = refs[:-1], refs[-1]
    rows, columns = outs[0].shape
    all_ref[...] = far_sum(
        devices, pl.program_id(0) * columns, columns, lines_ref, high_ref, low_ref
    )
    for k in range(devices):
        start = pl.multiple_of((me_ref[0] + devices - k) % devices * rows, rows)
        outs[k][...] = all_ref[pl.ds(start, rows), :]


def far_slopes(lines, high, low, me):
    devices, rows, width = lines.shape
    total_rows = devices * rows
    columns = COLUMNS
    whole = pl.BlockSpec((total_rows, width), lambda j, m: (0, 0))
    strip = pl.BlockSpec(memory_space=pltpu.VMEM)
    return pl.pallas_call(
        functools.partial(far_blocks_body, devices),
        grid_spec=pltpu.PrefetchScalarGridSpec(
            num_scalar_prefetch=1,
            grid=(width // columns,),
            in_specs=[whole, strip, strip],
            out_specs=[pl.BlockSpec((rows, columns), lambda j, m: (0, j))] * devices,
            scratch_shapes=[pltpu.VMEM((total_rows, columns), BF16)],
        ),
        out_shape=[jax.ShapeDtypeStruct((rows, width), BF16)] * devices,
        compiler_params=pltpu.CompilerParams(vmem_limit_bytes=20 * 2**20),
        cost_estimate=pl.CostEstimate(
            flops=4 * total_rows * (devices - 1) * width * width,
            bytes_accessed=4 * total_rows * width + 4 * high.size,
            transcendentals=0,
        ),
    )(me, lines.reshape(total_rows, width), high, low)


def local_body(base, field_ref, u_ref, w_ref, b_ref, below_ref, above_ref, strat_ref, high_ref, low_ref, out_ref, pad_ref):
    comp = base + pl.program_id(1)
    levels, width = out_ref.shape
    pad_ref[8 : 8 + levels, :] = field_ref[...].astype(F32)
    pad_ref[4:8, :] = below_ref[...].astype(F32)
    pad_ref[8 + levels : 12 + levels, :] = above_ref[...].astype(F32)
    is_w = (comp == 2).astype(F32)
    is_b = (comp == 3).astype(F32)
    strat = strat_ref[...] * is_b
    columns = COLUMNS
    for j in range(width // columns):
        here = slice(j * columns, (j + 1) * columns)
        near = dot(field_ref[...], panel(high_ref, j * columns, width, columns)) + dot(
            field_ref[...], panel(low_ref, j * columns, width, columns)
        )
        slope_z = None
        for offset in range(1, 5):
            term = STENCIL[offset - 1] * (
                pad_ref[8 + offset : 8 + offset + levels, here]
                - pad_ref[8 - offset : 8 - offset + levels, here]
            )
            slope_z = term if slope_z is None else slope_z + term
        speed_w = w_ref[:, here].astype(F32)
        out_ref[:, here] = (
            is_w * b_ref[:, here].astype(F32)
            - strat * speed_w
            - (u_ref[:, here].astype(F32) * near + speed_w * slope_z)
        )


def local_part(fields, below, above, strat_col, high, low, base, count, held):
    _, lines, levels, width = fields.shape

    def block(comp):
        return pl.BlockSpec(
            (None, None, levels, width),
            (lambda l, c: (base + c, l, 0, 0)) if comp is None else (lambda l, c: (comp, l, 0, 0)),
        )

    halo = pl.BlockSpec((None, None, 4, width), lambda l, c: (base + c, l, 0, 0))
    whole = pl.BlockSpec(memory_space=pltpu.VMEM)
    return pl.pallas_call(
        functools.partial(local_body, base),
        grid=(lines, count),
        in_specs=[
            block(None),
            block(0),
            block(2),
            block(3),
            halo,
            halo,
            pl.BlockSpec((levels, 1), lambda l, c: (0, 0)),
            whole,
            whole,
        ],
        out_specs=pl.BlockSpec((None, None, levels, width), lambda l, c: (c, l, 0, 0)),
        out_shape=jax.ShapeDtypeStruct((held, lines, levels, width), F32),
        scratch_shapes=[pltpu.VMEM((levels + 16, width), F32)],
        compiler_params=pltpu.CompilerParams(vmem_limit_bytes=20 * 2**20),
        cost_estimate=pl.CostEstimate(
            flops=4 * count * lines * levels * width * width,
            bytes_accessed=8 * count * lines * levels * width,
            transcendentals=0,
        ),
    )(fields, fields, fields, fields, below, above, strat_col, high, low)


def finish_body(count, me_ref, part_ref, u_ref, *refs):
    fars, out_ref = refs[:count], refs[-1]
    for k, far_ref in enumerate(fars):

        @pl.when(pl.program_id(0) == k)
        def _(far_ref=far_ref):
            out_ref[...] = part_ref[...] - u_ref[...].astype(F32) * far_ref[...].astype(F32)


def finish(out, part, speed_u, offsets, fars, me, total_rows):
    devices = len(fars)
    rows, width = fars[0].shape
    u_blocks = speed_u.shape[0] // rows
    base = 0 if out is None else total_rows // rows - devices
    given = [] if out is None else [out]

    def owner(i, m):
        offset = offsets[-1]
        for index in range(devices - 1):
            offset = jnp.where(i == index, offsets[index], offset)
        return (m[0] + offset) % devices

    return pl.pallas_call(
        functools.partial(finish_body, devices),
        grid_spec=pltpu.PrefetchScalarGridSpec(
            num_scalar_prefetch=1,
            grid=(devices,),
            in_specs=[
                pl.BlockSpec((rows, width), lambda i, m: (owner(i, m), 0)),
                pl.BlockSpec((rows, width), lambda i, m: (owner(i, m) % u_blocks, 0)),
            ]
            + [pl.BlockSpec((rows, width), lambda i, m: (0, 0))] * devices
            + [pl.BlockSpec(memory_space=pl.ANY)] * len(given),
            out_specs=pl.BlockSpec((rows, width), lambda i, m: (base + owner(i, m), 0)),
        ),
        out_shape=jax.ShapeDtypeStruct((total_rows, width), F32),
        input_output_aliases={3 + devices: 0} if given else {},
        compiler_params=pltpu.CompilerParams(vmem_limit_bytes=UPDATE_VMEM),
        cost_estimate=pl.CostEstimate(
            flops=2 * devices * rows * width,
            bytes_accessed=12 * devices * rows * width,
            transcendentals=0,
        ),
    )(me, part, speed_u, *fars, *given)


def order_of(devices):
    return sorted(range(1, devices), key=lambda k: abs(2 * k - devices))


def halos(fields):
    count = lax.axis_size("gz")
    forward = [(i, i + 1) for i in range(count - 1)]
    backward = [(target, source) for source, target in forward]
    levels = fields.shape[2]
    below = lax.ppermute(fields[:, :, levels - 4 :], "gz", forward)
    above = lax.ppermute(fields[:, :, :4], "gz", backward)
    return below, above


def body(fields, strat_sq):
    comps, lines, levels, width = fields.shape
    devices = lax.axis_size("gx")
    group = comps // 2
    shape = (devices, group * lines * levels // devices, width)
    me = lax.axis_index("gx").astype(jnp.int32)[None]

    def exchange(whole):
        return lax.all_to_all(whole, "gx", split_axis=0, concat_axis=0, tiled=True)

    def ahead(block, k):
        return lax.ppermute(block, "gx", [(i, (i + k) % devices) for i in range(devices)])

    first = exchange(fields[:group].reshape(shape))
    below, above = halos(fields)
    high, low = strips(devices * width, width)
    local = (fields, below, above, strat_sq[:, None], high, low)
    early = local_part(*local, 0, group, group)
    part = local_part(*local, group, group, group)
    source, early, part = lax.optimization_barrier((fields, early, part))
    speed_u = source[0].reshape(lines * levels, width)
    second = exchange(source[group:].reshape(shape))
    order = order_of(devices)
    held = group * lines * levels

    def back(outs, k):
        return ahead(outs[k], devices - k)

    outs, second = lax.optimization_barrier((far_slopes(first, high, low, me), second))
    fars = [outs[0]] + [back(outs, k) for k in order]
    later = list(far_slopes(second, high, low, me))
    last = [later[0]]
    for i, k in enumerate(order):
        later[k], fars[1 + i] = lax.optimization_barrier((later[k], fars[1 + i]))
        last.append(back(later, k))
    shape_flat = (held, width)
    out = finish(None, early.reshape(shape_flat), speed_u, [0] + order, fars, me, 2 * held)
    out = finish(out, part.reshape(shape_flat), speed_u, [0] + order, last, me, 2 * held)
    return out.reshape(fields.shape)


def solution(mesh):
    placed = (P(None, None, "gz", "gx"), P("gz"))
    return jax.shard_map(
        body, mesh=mesh, in_specs=placed, out_specs=P(None, None, "gz", "gx"), check_vma=False
    )
```

```python
import functools
import math

import jax
import jax.numpy as jnp
import numpy as np
from jax import lax
from jax.experimental import pallas as pl
from jax.experimental.pallas import tpu as pltpu
from jax.sharding import PartitionSpec as P

STENCIL = (4.0 / 5.0, -1.0 / 5.0, 4.0 / 105.0, -1.0 / 280.0)
BAND = 128
COLUMNS = 256
UPDATE_VMEM = 16 * 2**20
F32 = jnp.float32
BF16 = jnp.bfloat16


def kernel_row(length):
    index = np.arange(length)
    signed = np.where(index < length // 2, index, index - length).astype(np.float64)
    angle = np.pi * np.where(signed == 0, 1.0, signed) / length
    row = np.where(index % 2 == 0, 1.0, -1.0) * (np.pi / length) / np.tan(angle)
    row = np.where((index == 0) | (index == length // 2), 0.0, row)
    return jnp.asarray(row.astype(np.float32))[None, :]


def strip_body(pad, row_ref, high_ref, low_ref, run_ref):
    rows, length = run_ref.shape

    @pl.when(pl.program_id(0) == 0)
    def _():
        wide = jnp.broadcast_to(row_ref[...], (rows, length))
        run_ref[...] = pltpu.roll(wide, pad, 1, stride=1, stride_axis=0)

    @pl.when(pl.program_id(0) > 0)
    def _():
        run_ref[...] = pltpu.roll(run_ref[...], rows, 1)

    run = run_ref[...]
    high = run.astype(BF16)
    low = (run - high.astype(F32)).astype(BF16)
    high_ref[:, :length] = high
    low_ref[:, :length] = low
    if pad:
        high_ref[:, length:] = high[:, :pad]
        low_ref[:, length:] = low[:, :pad]


def strips(length, width):
    pad = width - BAND
    rows = 16
    shape = jax.ShapeDtypeStruct((BAND, length + pad), BF16)
    spec = pl.BlockSpec((rows, length + pad), lambda i: (i, 0))
    return pl.pallas_call(
        functools.partial(strip_body, pad),
        grid=(BAND // rows,),
        in_specs=[pl.BlockSpec((1, length), lambda i: (0, 0))],
        out_specs=[spec, spec],
        out_shape=[shape, shape],
        scratch_shapes=[pltpu.VMEM((rows, length), F32)],
        compiler_params=pltpu.CompilerParams(vmem_limit_bytes=8 * 2**20),
        cost_estimate=pl.CostEstimate(
            flops=4 * BAND * length, bytes_accessed=4 * BAND * length, transcendentals=0
        ),
    )(kernel_row(length))


def panel(strip_ref, first, width, columns):
    runs = [
        strip_ref[:, pl.ds(pl.multiple_of(first + width - BAND - BAND * i, BAND), columns)]
        for i in range(width // BAND)
    ]
    return runs[0] if len(runs) == 1 else jnp.concatenate(runs, axis=0)


def dot(left, right):
    return jnp.dot(left, right, preferred_element_type=F32)


def far_sum(devices, column, columns, lines_ref, high_ref, low_ref):
    total_rows, width = lines_ref.shape
    rows = total_rows // devices
    total = None
    for step in range(1, devices):
        cut = (devices - step) * rows
        moved = jnp.concatenate([lines_ref[cut:, :], lines_ref[:cut, :]], axis=0)
        first = step * width + column
        for strip_ref in (high_ref, low_ref):
            part = dot(moved, panel(strip_ref, first, width, columns))
            total = part if total is None else total + part
    return total.astype(BF16)


def far_whole_body(devices, me_ref, lines_ref, high_ref, low_ref, *refs):
    outs, all_ref = refs[:-1], refs[-1]
    rows, columns = outs[0].shape
    all_ref[...] = far_sum(
        devices, pl.program_id(0) * columns, columns, lines_ref, high_ref, low_ref
    )
    for k in range(devices):
        start = pl.multiple_of((me_ref[0] + devices - k) % devices * rows, rows)
        outs[k][...] = all_ref[pl.ds(start, rows), :]


def far_whole(lines, high, low, me):
    devices, rows, width = lines.shape
    total_rows = devices * rows
    columns = COLUMNS
    whole = pl.BlockSpec((total_rows, width), lambda j, m: (0, 0))
    strip = pl.BlockSpec(memory_space=pltpu.VMEM)
    return pl.pallas_call(
        functools.partial(far_whole_body, devices),
        grid_spec=pltpu.PrefetchScalarGridSpec(
            num_scalar_prefetch=1,
            grid=(width // columns,),
            in_specs=[whole, strip, strip],
            out_specs=[pl.BlockSpec((rows, columns), lambda j, m: (0, j))] * devices,
            scratch_shapes=[pltpu.VMEM((total_rows, columns), BF16)],
        ),
        out_shape=[jax.ShapeDtypeStruct((rows, width), BF16)] * devices,
        compiler_params=pltpu.CompilerParams(vmem_limit_bytes=20 * 2**20),
        cost_estimate=pl.CostEstimate(
            flops=4 * total_rows * (devices - 1) * width * width,
            bytes_accessed=4 * total_rows * width + 4 * high.size,
            transcendentals=0,
        ),
    )(me, lines.reshape(total_rows, width), high, low)


def far_body(devices, shifts, me_ref, *refs):
    sources = dict(zip([0] + shifts, refs[:devices]))
    high_ref, low_ref, outs = refs[devices], refs[devices + 1], refs[devices + 2 :]
    rows, width = sources[0].shape
    columns = outs[0].shape[1]
    column = pl.program_id(0) * columns
    total = None
    for step in range(1, devices):
        moved = jnp.concatenate(
            [sources[(step + target) % devices][...] for target in range(devices)], axis=0
        )
        first = step * width + column
        for strip_ref in (high_ref, low_ref):
            part = dot(moved, panel(strip_ref, first, width, columns))
            total = part if total is None else total + part
    for target in range(devices):
        outs[target][...] = total[target * rows : (target + 1) * rows, :].astype(BF16)


def far_slopes(flat, chunk, received, high, low, me):
    devices = len(received) + 1
    shifts = list(received)
    rows, width = received[1].shape
    columns = COLUMNS
    whole = pl.BlockSpec((rows, width), lambda j, m: (0, 0))
    strip = pl.BlockSpec(memory_space=pltpu.VMEM)
    return pl.pallas_call(
        functools.partial(far_body, devices, shifts),
        grid_spec=pltpu.PrefetchScalarGridSpec(
            num_scalar_prefetch=1,
            grid=(width // columns,),
            in_specs=[pl.BlockSpec((rows, width), lambda j, m: (chunk * devices + m[0], 0))]
            + [whole] * (devices - 1)
            + [strip] * 2,
            out_specs=[pl.BlockSpec((rows, columns), lambda j, m: (0, j))] * devices,
        ),
        out_shape=[jax.ShapeDtypeStruct((rows, width), BF16)] * devices,
        compiler_params=pltpu.CompilerParams(vmem_limit_bytes=20 * 2**20),
        cost_estimate=pl.CostEstimate(
            flops=4 * rows * devices * (devices - 1) * width * width,
            bytes_accessed=4 * rows * devices * width + 4 * high.size,
            transcendentals=0,
        ),
    )(me, flat, *received.values(), high, low)


def local_body(base, field_ref, u_ref, w_ref, b_ref, below_ref, above_ref, strat_ref, high_ref, low_ref, out_ref, pad_ref):
    comp = base + pl.program_id(1)
    levels, width = out_ref.shape
    pad_ref[8 : 8 + levels, :] = field_ref[...].astype(F32)
    pad_ref[4:8, :] = below_ref[...].astype(F32)
    pad_ref[8 + levels : 12 + levels, :] = above_ref[...].astype(F32)
    is_w = (comp == 2).astype(F32)
    is_b = (comp == 3).astype(F32)
    strat = strat_ref[...] * is_b
    columns = COLUMNS
    for j in range(width // columns):
        here = slice(j * columns, (j + 1) * columns)
        near = dot(field_ref[...], panel(high_ref, j * columns, width, columns)) + dot(
            field_ref[...], panel(low_ref, j * columns, width, columns)
        )
        slope_z = None
        for offset in range(1, 5):
            term = STENCIL[offset - 1] * (
                pad_ref[8 + offset : 8 + offset + levels, here]
                - pad_ref[8 - offset : 8 - offset + levels, here]
            )
            slope_z = term if slope_z is None else slope_z + term
        speed_w = w_ref[:, here].astype(F32)
        out_ref[:, here] = (
            is_w * b_ref[:, here].astype(F32)
            - strat * speed_w
            - (u_ref[:, here].astype(F32) * near + speed_w * slope_z)
        )


def local_part(fields, below, above, strat_col, high, low, base, count, held):
    _, lines, levels, width = fields.shape

    def block(comp):
        return pl.BlockSpec(
            (None, None, levels, width),
            (lambda l, c: (base + c, l, 0, 0)) if comp is None else (lambda l, c: (comp, l, 0, 0)),
        )

    halo = pl.BlockSpec((None, None, 4, width), lambda l, c: (base + c, l, 0, 0))
    whole = pl.BlockSpec(memory_space=pltpu.VMEM)
    return pl.pallas_call(
        functools.partial(local_body, base),
        grid=(lines, count),
        in_specs=[
            block(None),
            block(0),
            block(2),
            block(3),
            halo,
            halo,
            pl.BlockSpec((levels, 1), lambda l, c: (0, 0)),
            whole,
            whole,
        ],
        out_specs=pl.BlockSpec((None, None, levels, width), lambda l, c: (c, l, 0, 0)),
        out_shape=jax.ShapeDtypeStruct((held, lines, levels, width), F32),
        scratch_shapes=[pltpu.VMEM((levels + 16, width), F32)],
        compiler_params=pltpu.CompilerParams(vmem_limit_bytes=20 * 2**20),
        cost_estimate=pl.CostEstimate(
            flops=4 * count * lines * levels * width * width,
            bytes_accessed=8 * count * lines * levels * width,
            transcendentals=0,
        ),
    )(fields, fields, fields, fields, below, above, strat_col, high, low)


def finish_body(count, me_ref, part_ref, u_ref, *refs):
    fars, out_ref = refs[:count], refs[-1]
    for k, far_ref in enumerate(fars):

        @pl.when(pl.program_id(0) == k)
        def _(far_ref=far_ref):
            out_ref[...] = part_ref[...] - u_ref[...].astype(F32) * far_ref[...].astype(F32)


def finish(out, part, speed_u, offsets, fars, me, total_rows):
    devices = len(fars)
    rows, width = fars[0].shape
    u_blocks = speed_u.shape[0] // rows
    base = 0 if out is None else total_rows // rows - devices
    given = [] if out is None else [out]

    def owner(i, m):
        offset = offsets[-1]
        for index in range(devices - 1):
            offset = jnp.where(i == index, offsets[index], offset)
        return (m[0] + offset) % devices

    return pl.pallas_call(
        functools.partial(finish_body, devices),
        grid_spec=pltpu.PrefetchScalarGridSpec(
            num_scalar_prefetch=1,
            grid=(devices,),
            in_specs=[
                pl.BlockSpec((rows, width), lambda i, m: (owner(i, m), 0)),
                pl.BlockSpec((rows, width), lambda i, m: (owner(i, m) % u_blocks, 0)),
            ]
            + [pl.BlockSpec((rows, width), lambda i, m: (0, 0))] * devices
            + [pl.BlockSpec(memory_space=pl.ANY)] * len(given),
            out_specs=pl.BlockSpec((rows, width), lambda i, m: (base + owner(i, m), 0)),
        ),
        out_shape=jax.ShapeDtypeStruct((total_rows, width), F32),
        input_output_aliases={3 + devices: 0} if given else {},
        compiler_params=pltpu.CompilerParams(vmem_limit_bytes=UPDATE_VMEM),
        cost_estimate=pl.CostEstimate(
            flops=2 * devices * rows * width,
            bytes_accessed=12 * devices * rows * width,
            transcendentals=0,
        ),
    )(me, part, speed_u, *fars, *given)


def order_of(devices):
    return sorted(range(1, devices), key=lambda k: abs(2 * k - devices))


def halos(fields):
    count = lax.axis_size("gz")
    forward = [(i, i + 1) for i in range(count - 1)]
    backward = [(target, source) for source, target in forward]
    levels = fields.shape[2]
    below = lax.ppermute(fields[:, :, levels - 4 :], "gz", forward)
    above = lax.ppermute(fields[:, :, :4], "gz", backward)
    return below, above


def after(value, *others):
    return lax.optimization_barrier((value, others))[0]


def body(fields, strat_sq):
    comps, lines, levels, width = fields.shape
    devices = lax.axis_size("gx")
    group = comps // 2
    held = group * lines * levels
    rows = held // devices
    index = lax.axis_index("gx").astype(jnp.int32)
    me = index[None]
    flat = fields.reshape(2 * held, width)
    order = order_of(devices)
    shifts = range(1, devices)

    def ahead(block, k):
        return lax.ppermute(block, "gx", [(i, (i + k) % devices) for i in range(devices)])

    def block_of(source, chunk, k):
        start = (chunk * devices + (index + k) % devices) * rows
        return lax.dynamic_slice_in_dim(source, start, rows, 0)

    first = lax.all_to_all(
        flat[:held].reshape(devices, rows, width), "gx", split_axis=0, concat_axis=0, tiled=True
    )
    below, above = halos(fields)
    high, low = strips(devices * width, width)
    local = (fields, below, above, strat_sq[:, None], high, low)
    early = local_part(*local, 0, group, group)
    part = local_part(*local, group, group, group)
    source, early, part, first = lax.optimization_barrier((flat, early, part, first))
    speed_u = source[: lines * levels]
    second = {k: ahead(block_of(source, 1, k), k) for k in order}
    outs = far_whole(first, high, low, me)
    outs, blocks = lax.optimization_barrier((outs, list(second.values())))
    second = dict(zip(second, blocks))
    later = far_slopes(flat, 1, second, high, low, me)
    back = {k: ahead(outs[k], devices - k) for k in shifts}
    last = {k: ahead(after(later[k], back[k]), devices - k) for k in shifts}
    offsets = [0] + order
    fars = [outs[0]] + [back[k] for k in order]
    out = finish(None, early.reshape(held, width), speed_u, offsets, fars, me, 2 * held)
    fars = [later[0]] + [last[k] for k in order]
    out = finish(out, part.reshape(held, width), speed_u, offsets, fars, me, 2 * held)
    return out.reshape(fields.shape)


def solution(mesh):
    placed = (P(None, None, "gz", "gx"), P("gz"))
    return jax.shard_map(
        body, mesh=mesh, in_specs=placed, out_specs=P(None, None, "gz", "gx"), check_vma=False
    )
```

```python
import functools
import math

import jax
import jax.numpy as jnp
import numpy as np
from jax import lax
from jax.experimental import pallas as pl
from jax.experimental.pallas import tpu as pltpu
from jax.sharding import PartitionSpec as P

STENCIL = (4.0 / 5.0, -1.0 / 5.0, 4.0 / 105.0, -1.0 / 280.0)
BAND = 128
COLUMNS = 256
UPDATE_VMEM = 16 * 2**20
F32 = jnp.float32
BF16 = jnp.bfloat16


def kernel_row(length):
    index = np.arange(length)
    signed = np.where(index < length // 2, index, index - length).astype(np.float64)
    angle = np.pi * np.where(signed == 0, 1.0, signed) / length
    row = np.where(index % 2 == 0, 1.0, -1.0) * (np.pi / length) / np.tan(angle)
    row = np.where((index == 0) | (index == length // 2), 0.0, row)
    return jnp.asarray(row.astype(np.float32))[None, :]


def strip_body(pad, row_ref, high_ref, low_ref, run_ref):
    rows, length = run_ref.shape

    @pl.when(pl.program_id(0) == 0)
    def _():
        wide = jnp.broadcast_to(row_ref[...], (rows, length))
        run_ref[...] = pltpu.roll(wide, pad, 1, stride=1, stride_axis=0)

    @pl.when(pl.program_id(0) > 0)
    def _():
        run_ref[...] = pltpu.roll(run_ref[...], rows, 1)

    run = run_ref[...]
    high = run.astype(BF16)
    low = (run - high.astype(F32)).astype(BF16)
    high_ref[:, :length] = high
    low_ref[:, :length] = low
    if pad:
        high_ref[:, length:] = high[:, :pad]
        low_ref[:, length:] = low[:, :pad]


def strips(length, width):
    pad = width - BAND
    rows = 16
    shape = jax.ShapeDtypeStruct((BAND, length + pad), BF16)
    spec = pl.BlockSpec((rows, length + pad), lambda i: (i, 0))
    return pl.pallas_call(
        functools.partial(strip_body, pad),
        grid=(BAND // rows,),
        in_specs=[pl.BlockSpec((1, length), lambda i: (0, 0))],
        out_specs=[spec, spec],
        out_shape=[shape, shape],
        scratch_shapes=[pltpu.VMEM((rows, length), F32)],
        compiler_params=pltpu.CompilerParams(vmem_limit_bytes=8 * 2**20),
        cost_estimate=pl.CostEstimate(
            flops=4 * BAND * length, bytes_accessed=4 * BAND * length, transcendentals=0
        ),
    )(kernel_row(length))


def panel(strip_ref, first, width, columns):
    runs = [
        strip_ref[:, pl.ds(pl.multiple_of(first + width - BAND - BAND * i, BAND), columns)]
        for i in range(width // BAND)
    ]
    return runs[0] if len(runs) == 1 else jnp.concatenate(runs, axis=0)


def dot(left, right):
    return jnp.dot(left, right, preferred_element_type=F32)


def far_sum(devices, column, columns, lines_ref, high_ref, low_ref):
    total_rows, width = lines_ref.shape
    rows = total_rows // devices
    total = None
    for step in range(1, devices):
        cut = (devices - step) * rows
        moved = jnp.concatenate([lines_ref[cut:, :], lines_ref[:cut, :]], axis=0)
        first = step * width + column
        for strip_ref in (high_ref, low_ref):
            part = dot(moved, panel(strip_ref, first, width, columns))
            total = part if total is None else total + part
    return total.astype(BF16)


def far_whole_body(devices, me_ref, lines_ref, high_ref, low_ref, *refs):
    outs, all_ref = refs[:-1], refs[-1]
    rows, columns = outs[0].shape
    all_ref[...] = far_sum(
        devices, pl.program_id(0) * columns, columns, lines_ref, high_ref, low_ref
    )
    for k in range(devices):
        start = pl.multiple_of((me_ref[0] + devices - k) % devices * rows, rows)
        outs[k][...] = all_ref[pl.ds(start, rows), :]


def far_whole(lines, high, low, me):
    devices, rows, width = lines.shape
    total_rows = devices * rows
    columns = COLUMNS
    whole = pl.BlockSpec((total_rows, width), lambda j, m: (0, 0))
    strip = pl.BlockSpec(memory_space=pltpu.VMEM)
    return pl.pallas_call(
        functools.partial(far_whole_body, devices),
        grid_spec=pltpu.PrefetchScalarGridSpec(
            num_scalar_prefetch=1,
            grid=(width // columns,),
            in_specs=[whole, strip, strip],
            out_specs=[pl.BlockSpec((rows, columns), lambda j, m: (0, j))] * devices,
            scratch_shapes=[pltpu.VMEM((total_rows, columns), BF16)],
        ),
        out_shape=[jax.ShapeDtypeStruct((rows, width), BF16)] * devices,
        compiler_params=pltpu.CompilerParams(vmem_limit_bytes=20 * 2**20),
        cost_estimate=pl.CostEstimate(
            flops=4 * total_rows * (devices - 1) * width * width,
            bytes_accessed=4 * total_rows * width + 4 * high.size,
            transcendentals=0,
        ),
    )(me, lines.reshape(total_rows, width), high, low)


def far_body(devices, shifts, me_ref, *refs):
    sources = dict(zip([0] + shifts, refs[:devices]))
    high_ref, low_ref, outs = refs[devices], refs[devices + 1], refs[devices + 2 :]
    rows, width = sources[0].shape
    columns = outs[0].shape[1]
    column = pl.program_id(0) * columns
    total = None
    for step in range(1, devices):
        moved = jnp.concatenate(
            [sources[(step + target) % devices][...] for target in range(devices)], axis=0
        )
        first = step * width + column
        for strip_ref in (high_ref, low_ref):
            part = dot(moved, panel(strip_ref, first, width, columns))
            total = part if total is None else total + part
    for target in range(devices):
        outs[target][...] = total[target * rows : (target + 1) * rows, :].astype(BF16)


def far_slopes(flat, chunk, received, high, low, me):
    devices = len(received) + 1
    shifts = list(received)
    rows, width = received[1].shape
    columns = COLUMNS
    whole = pl.BlockSpec((rows, width), lambda j, m: (0, 0))
    strip = pl.BlockSpec(memory_space=pltpu.VMEM)
    return pl.pallas_call(
        functools.partial(far_body, devices, shifts),
        grid_spec=pltpu.PrefetchScalarGridSpec(
            num_scalar_prefetch=1,
            grid=(width // columns,),
            in_specs=[pl.BlockSpec((rows, width), lambda j, m: (chunk * devices + m[0], 0))]
            + [whole] * (devices - 1)
            + [strip] * 2,
            out_specs=[pl.BlockSpec((rows, columns), lambda j, m: (0, j))] * devices,
        ),
        out_shape=[jax.ShapeDtypeStruct((rows, width), BF16)] * devices,
        compiler_params=pltpu.CompilerParams(vmem_limit_bytes=20 * 2**20),
        cost_estimate=pl.CostEstimate(
            flops=4 * rows * devices * (devices - 1) * width * width,
            bytes_accessed=4 * rows * devices * width + 4 * high.size,
            transcendentals=0,
        ),
    )(me, flat, *received.values(), high, low)


def local_body(base, field_ref, u_ref, w_ref, b_ref, below_ref, above_ref, strat_ref, high_ref, low_ref, out_ref, pad_ref):
    comp = base + pl.program_id(1)
    levels, width = out_ref.shape
    pad_ref[8 : 8 + levels, :] = field_ref[...].astype(F32)
    pad_ref[4:8, :] = below_ref[...].astype(F32)
    pad_ref[8 + levels : 12 + levels, :] = above_ref[...].astype(F32)
    is_w = (comp == 2).astype(F32)
    is_b = (comp == 3).astype(F32)
    strat = strat_ref[...] * is_b
    columns = COLUMNS
    for j in range(width // columns):
        here = slice(j * columns, (j + 1) * columns)
        near = dot(field_ref[...], panel(high_ref, j * columns, width, columns)) + dot(
            field_ref[...], panel(low_ref, j * columns, width, columns)
        )
        slope_z = None
        for offset in range(1, 5):
            term = STENCIL[offset - 1] * (
                pad_ref[8 + offset : 8 + offset + levels, here]
                - pad_ref[8 - offset : 8 - offset + levels, here]
            )
            slope_z = term if slope_z is None else slope_z + term
        speed_w = w_ref[:, here].astype(F32)
        out_ref[:, here] = (
            is_w * b_ref[:, here].astype(F32)
            - strat * speed_w
            - (u_ref[:, here].astype(F32) * near + speed_w * slope_z)
        )


def local_part(fields, below, above, strat_col, high, low, base, count, held):
    _, lines, levels, width = fields.shape

    def block(comp):
        return pl.BlockSpec(
            (None, None, levels, width),
            (lambda l, c: (base + c, l, 0, 0)) if comp is None else (lambda l, c: (comp, l, 0, 0)),
        )

    halo = pl.BlockSpec((None, None, 4, width), lambda l, c: (base + c, l, 0, 0))
    whole = pl.BlockSpec(memory_space=pltpu.VMEM)
    return pl.pallas_call(
        functools.partial(local_body, base),
        grid=(lines, count),
        in_specs=[
            block(None),
            block(0),
            block(2),
            block(3),
            halo,
            halo,
            pl.BlockSpec((levels, 1), lambda l, c: (0, 0)),
            whole,
            whole,
        ],
        out_specs=pl.BlockSpec((None, None, levels, width), lambda l, c: (c, l, 0, 0)),
        out_shape=jax.ShapeDtypeStruct((held, lines, levels, width), F32),
        scratch_shapes=[pltpu.VMEM((levels + 16, width), F32)],
        compiler_params=pltpu.CompilerParams(vmem_limit_bytes=20 * 2**20),
        cost_estimate=pl.CostEstimate(
            flops=4 * count * lines * levels * width * width,
            bytes_accessed=8 * count * lines * levels * width,
            transcendentals=0,
        ),
    )(fields, fields, fields, fields, below, above, strat_col, high, low)


def finish_body(offsets, base, me_ref, part_ref, u_ref, *refs):
    devices = len(offsets)
    fars, out_ref, sum_ref, sems = refs[:devices], refs[-3], refs[-2], refs[-1]
    rows, _ = fars[0].shape
    u_blocks = u_ref.shape[0] // rows
    copies = []
    for i, (offset, far_ref) in enumerate(zip(offsets, fars)):
        owner = (me_ref[0] + offset) % devices
        part = part_ref[pl.ds(pl.multiple_of(owner * rows, rows), rows), :]
        speed_u = u_ref[pl.ds(pl.multiple_of(owner % u_blocks * rows, rows), rows), :]
        sum_ref[i] = part - speed_u.astype(F32) * far_ref[...].astype(F32)
        target = pl.multiple_of((base + owner) * rows, rows)
        copies.append(
            pltpu.make_async_copy(sum_ref.at[i], out_ref.at[pl.ds(target, rows)], sems.at[i])
        )
        copies[-1].start()
    for copy in copies:
        copy.wait()


def finish(out, part, speed_u, offsets, fars, me, total_rows):
    devices = len(fars)
    rows, width = fars[0].shape
    base = 0 if out is None else total_rows // rows - devices
    given = [] if out is None else [out]
    return pl.pallas_call(
        functools.partial(finish_body, offsets, base),
        in_specs=[pl.BlockSpec(memory_space=pltpu.SMEM)]
        + [pl.BlockSpec(memory_space=pltpu.VMEM)] * (2 + devices)
        + [pl.BlockSpec(memory_space=pl.ANY)] * len(given),
        out_specs=pl.BlockSpec(memory_space=pl.ANY),
        out_shape=jax.ShapeDtypeStruct((total_rows, width), F32),
        scratch_shapes=[
            pltpu.VMEM((devices, rows, width), F32),
            pltpu.SemaphoreType.DMA((devices,)),
        ],
        input_output_aliases={3 + devices: 0} if given else {},
        compiler_params=pltpu.CompilerParams(vmem_limit_bytes=UPDATE_VMEM),
        cost_estimate=pl.CostEstimate(
            flops=2 * devices * rows * width,
            bytes_accessed=12 * devices * rows * width,
            transcendentals=0,
        ),
    )(me, part, speed_u, *fars, *given)


def order_of(devices):
    return sorted(range(1, devices), key=lambda k: abs(2 * k - devices))


def halos(fields):
    count = lax.axis_size("gz")
    forward = [(i, i + 1) for i in range(count - 1)]
    backward = [(target, source) for source, target in forward]
    levels = fields.shape[2]
    below = lax.ppermute(fields[:, :, levels - 4 :], "gz", forward)
    above = lax.ppermute(fields[:, :, :4], "gz", backward)
    return below, above


def after(value, *others):
    return lax.optimization_barrier((value, others))[0]


def body(fields, strat_sq):
    comps, lines, levels, width = fields.shape
    devices = lax.axis_size("gx")
    group = comps // 2
    held = group * lines * levels
    rows = held // devices
    index = lax.axis_index("gx").astype(jnp.int32)
    me = index[None]
    flat = fields.reshape(2 * held, width)
    order = order_of(devices)
    shifts = range(1, devices)

    def ahead(block, k):
        return lax.ppermute(block, "gx", [(i, (i + k) % devices) for i in range(devices)])

    def block_of(source, chunk, k):
        start = (chunk * devices + (index + k) % devices) * rows
        return lax.dynamic_slice_in_dim(source, start, rows, 0)

    first = lax.all_to_all(
        flat[:held].reshape(devices, rows, width), "gx", split_axis=0, concat_axis=0, tiled=True
    )
    below, above = halos(fields)
    high, low = strips(devices * width, width)
    local = (fields, below, above, strat_sq[:, None], high, low)
    early = local_part(*local, 0, group, group)
    part = local_part(*local, group, group, group)
    source, early, part, first = lax.optimization_barrier((flat, early, part, first))
    speed_u = source[: lines * levels]
    second = {k: ahead(block_of(source, 1, k), k) for k in order}
    outs = far_whole(first, high, low, me)
    outs, blocks = lax.optimization_barrier((outs, list(second.values())))
    second = dict(zip(second, blocks))
    later = far_slopes(flat, 1, second, high, low, me)
    back = {k: ahead(outs[k], devices - k) for k in shifts}
    last = {k: ahead(after(later[k], back[k]), devices - k) for k in shifts}
    offsets = [0] + order
    fars = [outs[0]] + [back[k] for k in order]
    out = finish(None, early.reshape(held, width), speed_u, offsets, fars, me, 2 * held)
    fars = [later[0]] + [last[k] for k in order]
    out = finish(out, part.reshape(held, width), speed_u, offsets, fars, me, 2 * held)
    return out.reshape(fields.shape)


def solution(mesh):
    placed = (P(None, None, "gz", "gx"), P("gz"))
    return jax.shard_map(
        body, mesh=mesh, in_specs=placed, out_specs=P(None, None, "gz", "gx"), check_vma=False
    )
```

```python
import functools
import math

import jax
import jax.numpy as jnp
import numpy as np
from jax import lax
from jax.experimental import pallas as pl
from jax.experimental.pallas import tpu as pltpu
from jax.sharding import PartitionSpec as P

STENCIL = (4.0 / 5.0, -1.0 / 5.0, 4.0 / 105.0, -1.0 / 280.0)
BAND = 128
COLUMNS = 256
UPDATE_VMEM = 16 * 2**20
F32 = jnp.float32
BF16 = jnp.bfloat16


def kernel_row(length):
    index = np.arange(length)
    signed = np.where(index < length // 2, index, index - length).astype(np.float64)
    angle = np.pi * np.where(signed == 0, 1.0, signed) / length
    row = np.where(index % 2 == 0, 1.0, -1.0) * (np.pi / length) / np.tan(angle)
    row = np.where((index == 0) | (index == length // 2), 0.0, row)
    return jnp.asarray(row.astype(np.float32))[None, :]


def strip_body(pad, row_ref, high_ref, low_ref, run_ref):
    rows, length = run_ref.shape

    @pl.when(pl.program_id(0) == 0)
    def _():
        wide = jnp.broadcast_to(row_ref[...], (rows, length))
        run_ref[...] = pltpu.roll(wide, pad, 1, stride=1, stride_axis=0)

    @pl.when(pl.program_id(0) > 0)
    def _():
        run_ref[...] = pltpu.roll(run_ref[...], rows, 1)

    run = run_ref[...]
    high = run.astype(BF16)
    low = (run - high.astype(F32)).astype(BF16)
    high_ref[:, :length] = high
    low_ref[:, :length] = low
    if pad:
        high_ref[:, length:] = high[:, :pad]
        low_ref[:, length:] = low[:, :pad]


def strips(length, width):
    pad = width - BAND
    rows = 16
    shape = jax.ShapeDtypeStruct((BAND, length + pad), BF16)
    spec = pl.BlockSpec((rows, length + pad), lambda i: (i, 0))
    return pl.pallas_call(
        functools.partial(strip_body, pad),
        grid=(BAND // rows,),
        in_specs=[pl.BlockSpec((1, length), lambda i: (0, 0))],
        out_specs=[spec, spec],
        out_shape=[shape, shape],
        scratch_shapes=[pltpu.VMEM((rows, length), F32)],
        compiler_params=pltpu.CompilerParams(vmem_limit_bytes=8 * 2**20),
        cost_estimate=pl.CostEstimate(
            flops=4 * BAND * length, bytes_accessed=4 * BAND * length, transcendentals=0
        ),
    )(kernel_row(length))


def panel(strip_ref, first, width, columns):
    runs = [
        strip_ref[:, pl.ds(pl.multiple_of(first + width - BAND - BAND * i, BAND), columns)]
        for i in range(width // BAND)
    ]
    return runs[0] if len(runs) == 1 else jnp.concatenate(runs, axis=0)


def dot(left, right):
    return jnp.dot(left, right, preferred_element_type=F32)


def far_sum(devices, column, columns, lines_ref, high_ref, low_ref):
    total_rows, width = lines_ref.shape
    rows = total_rows // devices
    total = None
    for step in range(1, devices):
        cut = (devices - step) * rows
        moved = jnp.concatenate([lines_ref[cut:, :], lines_ref[:cut, :]], axis=0)
        first = step * width + column
        for strip_ref in (high_ref, low_ref):
            part = dot(moved, panel(strip_ref, first, width, columns))
            total = part if total is None else total + part
    return total.astype(BF16)


def far_whole_body(devices, me_ref, lines_ref, high_ref, low_ref, *refs):
    outs, all_ref = refs[:-1], refs[-1]
    rows, columns = outs[0].shape
    all_ref[...] = far_sum(
        devices, pl.program_id(0) * columns, columns, lines_ref, high_ref, low_ref
    )
    for k in range(devices):
        start = pl.multiple_of((me_ref[0] + devices - k) % devices * rows, rows)
        outs[k][...] = all_ref[pl.ds(start, rows), :]


def far_whole(lines, high, low, me):
    devices, rows, width = lines.shape
    total_rows = devices * rows
    columns = COLUMNS
    whole = pl.BlockSpec((total_rows, width), lambda j, m: (0, 0))
    strip = pl.BlockSpec(memory_space=pltpu.VMEM)
    return pl.pallas_call(
        functools.partial(far_whole_body, devices),
        grid_spec=pltpu.PrefetchScalarGridSpec(
            num_scalar_prefetch=1,
            grid=(width // columns,),
            in_specs=[whole, strip, strip],
            out_specs=[pl.BlockSpec((rows, columns), lambda j, m: (0, j))] * devices,
            scratch_shapes=[pltpu.VMEM((total_rows, columns), BF16)],
        ),
        out_shape=[jax.ShapeDtypeStruct((rows, width), BF16)] * devices,
        compiler_params=pltpu.CompilerParams(vmem_limit_bytes=20 * 2**20),
        cost_estimate=pl.CostEstimate(
            flops=4 * total_rows * (devices - 1) * width * width,
            bytes_accessed=4 * total_rows * width + 4 * high.size,
            transcendentals=0,
        ),
    )(me, lines.reshape(total_rows, width), high, low)


def far_body(devices, shifts, me_ref, *refs):
    sources = dict(zip([0] + shifts, refs[:devices]))
    high_ref, low_ref, outs = refs[devices], refs[devices + 1], refs[devices + 2 :]
    rows, width = sources[0].shape
    columns = outs[0].shape[1]
    column = pl.program_id(0) * columns
    total = None
    for step in range(1, devices):
        moved = jnp.concatenate(
            [sources[(step + target) % devices][...] for target in range(devices)], axis=0
        )
        first = step * width + column
        for strip_ref in (high_ref, low_ref):
            part = dot(moved, panel(strip_ref, first, width, columns))
            total = part if total is None else total + part
    for target in range(devices):
        outs[target][...] = total[target * rows : (target + 1) * rows, :].astype(BF16)


def far_slopes(flat, chunk, received, high, low, me):
    devices = len(received) + 1
    shifts = list(received)
    rows, width = received[1].shape
    columns = COLUMNS
    whole = pl.BlockSpec((rows, width), lambda j, m: (0, 0))
    strip = pl.BlockSpec(memory_space=pltpu.VMEM)
    return pl.pallas_call(
        functools.partial(far_body, devices, shifts),
        grid_spec=pltpu.PrefetchScalarGridSpec(
            num_scalar_prefetch=1,
            grid=(width // columns,),
            in_specs=[pl.BlockSpec((rows, width), lambda j, m: (chunk * devices + m[0], 0))]
            + [whole] * (devices - 1)
            + [strip] * 2,
            out_specs=[pl.BlockSpec((rows, columns), lambda j, m: (0, j))] * devices,
        ),
        out_shape=[jax.ShapeDtypeStruct((rows, width), BF16)] * devices,
        compiler_params=pltpu.CompilerParams(vmem_limit_bytes=20 * 2**20),
        cost_estimate=pl.CostEstimate(
            flops=4 * rows * devices * (devices - 1) * width * width,
            bytes_accessed=4 * rows * devices * width + 4 * high.size,
            transcendentals=0,
        ),
    )(me, flat, *received.values(), high, low)


def local_body(base, field_ref, u_ref, w_ref, b_ref, below_ref, above_ref, strat_ref, high_ref, low_ref, out_ref, pad_ref):
    comp = base + pl.program_id(1)
    levels, width = out_ref.shape
    pad_ref[8 : 8 + levels, :] = field_ref[...].astype(F32)
    pad_ref[4:8, :] = below_ref[...].astype(F32)
    pad_ref[8 + levels : 12 + levels, :] = above_ref[...].astype(F32)
    is_w = (comp == 2).astype(F32)
    is_b = (comp == 3).astype(F32)
    strat = strat_ref[...] * is_b
    columns = COLUMNS
    for j in range(width // columns):
        here = slice(j * columns, (j + 1) * columns)
        near = dot(field_ref[...], panel(high_ref, j * columns, width, columns)) + dot(
            field_ref[...], panel(low_ref, j * columns, width, columns)
        )
        slope_z = None
        for offset in range(1, 5):
            term = STENCIL[offset - 1] * (
                pad_ref[8 + offset : 8 + offset + levels, here]
                - pad_ref[8 - offset : 8 - offset + levels, here]
            )
            slope_z = term if slope_z is None else slope_z + term
        speed_w = w_ref[:, here].astype(F32)
        out_ref[:, here] = (
            is_w * b_ref[:, here].astype(F32)
            - strat * speed_w
            - (u_ref[:, here].astype(F32) * near + speed_w * slope_z)
        )


def local_part(fields, below, above, strat_col, high, low, base, count, held):
    _, lines, levels, width = fields.shape

    def block(comp):
        return pl.BlockSpec(
            (None, None, levels, width),
            (lambda l, c: (base + c, l, 0, 0)) if comp is None else (lambda l, c: (comp, l, 0, 0)),
        )

    halo = pl.BlockSpec((None, None, 4, width), lambda l, c: (base + c, l, 0, 0))
    whole = pl.BlockSpec(memory_space=pltpu.VMEM)
    return pl.pallas_call(
        functools.partial(local_body, base),
        grid=(lines, count),
        in_specs=[
            block(None),
            block(0),
            block(2),
            block(3),
            halo,
            halo,
            pl.BlockSpec((levels, 1), lambda l, c: (0, 0)),
            whole,
            whole,
        ],
        out_specs=pl.BlockSpec((None, None, levels, width), lambda l, c: (c, l, 0, 0)),
        out_shape=jax.ShapeDtypeStruct((held, lines, levels, width), F32),
        scratch_shapes=[pltpu.VMEM((levels + 16, width), F32)],
        compiler_params=pltpu.CompilerParams(vmem_limit_bytes=20 * 2**20),
        cost_estimate=pl.CostEstimate(
            flops=4 * count * lines * levels * width * width,
            bytes_accessed=8 * count * lines * levels * width,
            transcendentals=0,
        ),
    )(fields, fields, fields, fields, below, above, strat_col, high, low)


def finish_body(offsets, base, me_ref, part_ref, u_ref, *refs):
    devices = len(offsets)
    fars, out_ref, sum_ref, sems = refs[:devices], refs[-3], refs[-2], refs[-1]
    rows, _ = fars[0].shape
    u_blocks = u_ref.shape[0] // rows
    copies = []
    for i, (offset, far_ref) in enumerate(zip(offsets, fars)):
        owner = (me_ref[0] + offset) % devices
        part = part_ref[pl.ds(pl.multiple_of(owner * rows, rows), rows), :]
        speed_u = u_ref[pl.ds(pl.multiple_of(owner % u_blocks * rows, rows), rows), :]
        sum_ref[i] = part - speed_u.astype(F32) * far_ref[...].astype(F32)
        target = pl.multiple_of((base + owner) * rows, rows)
        copies.append(
            pltpu.make_async_copy(sum_ref.at[i], out_ref.at[pl.ds(target, rows)], sems.at[i])
        )
        copies[-1].start()
    for copy in copies:
        copy.wait()


def finish(out, part, speed_u, offsets, fars, me, total_rows):
    devices = len(fars)
    rows, width = fars[0].shape
    base = 0 if out is None else total_rows // rows - devices
    given = [] if out is None else [out]
    return pl.pallas_call(
        functools.partial(finish_body, offsets, base),
        in_specs=[pl.BlockSpec(memory_space=pltpu.SMEM)]
        + [pl.BlockSpec(memory_space=pltpu.VMEM)] * (2 + devices)
        + [pl.BlockSpec(memory_space=pl.ANY)] * len(given),
        out_specs=pl.BlockSpec(memory_space=pl.ANY),
        out_shape=jax.ShapeDtypeStruct((total_rows, width), F32),
        scratch_shapes=[
            pltpu.VMEM((devices, rows, width), F32),
            pltpu.SemaphoreType.DMA((devices,)),
        ],
        input_output_aliases={3 + devices: 0} if given else {},
        compiler_params=pltpu.CompilerParams(vmem_limit_bytes=UPDATE_VMEM),
        cost_estimate=pl.CostEstimate(
            flops=2 * devices * rows * width,
            bytes_accessed=12 * devices * rows * width,
            transcendentals=0,
        ),
    )(me, part, speed_u, *fars, *given)


def order_of(devices):
    return sorted(range(1, devices), key=lambda k: abs(2 * k - devices))


def halos(fields):
    count = lax.axis_size("gz")
    forward = [(i, i + 1) for i in range(count - 1)]
    backward = [(target, source) for source, target in forward]
    levels = fields.shape[2]
    below = lax.ppermute(fields[:, :, levels - 4 :], "gz", forward)
    above = lax.ppermute(fields[:, :, :4], "gz", backward)
    return below, above


def after(value, *others):
    return lax.optimization_barrier((value, others))[0]


def body(fields, strat_sq):
    comps, lines, levels, width = fields.shape
    devices = lax.axis_size("gx")
    group = comps // 2
    held = group * lines * levels
    rows = held // devices
    index = lax.axis_index("gx").astype(jnp.int32)
    me = index[None]
    flat = fields.reshape(2 * held, width)
    order = order_of(devices)
    shifts = range(1, devices)

    def ahead(block, k):
        return lax.ppermute(block, "gx", [(i, (i + k) % devices) for i in range(devices)])

    def block_of(source, chunk, k):
        start = (chunk * devices + (index + k) % devices) * rows
        return lax.dynamic_slice_in_dim(source, start, rows, 0)

    first = lax.all_to_all(
        flat[:held].reshape(devices, rows, width), "gx", split_axis=0, concat_axis=0, tiled=True
    )
    below, above = halos(fields)
    high, low = strips(devices * width, width)
    local = (fields, below, above, strat_sq[:, None], high, low)
    early = local_part(*local, 0, group, group)
    part = local_part(*local, group, group, group)
    source, early, part = lax.optimization_barrier((flat, early, part))
    speed_u = source[: lines * levels]
    near_first = order[::-1]
    cut = [block_of(source, 1, k) for k in near_first]
    cut, first = lax.optimization_barrier((cut, first))
    second = {k: ahead(block, k) for k, block in zip(near_first, cut)}
    outs = far_whole(first, high, low, me)
    outs, blocks = lax.optimization_barrier((outs, list(second.values())))
    second = dict(zip(second, blocks))
    later = far_slopes(flat, 1, second, high, low, me)
    back = {k: ahead(outs[k], devices - k) for k in shifts}
    last = {k: ahead(after(later[k], back[k]), devices - k) for k in shifts}
    offsets = [0] + order
    fars = [outs[0]] + [back[k] for k in order]
    out = finish(None, early.reshape(held, width), speed_u, offsets, fars, me, 2 * held)
    fars = [later[0]] + [last[k] for k in order]
    out = finish(out, part.reshape(held, width), speed_u, offsets, fars, me, 2 * held)
    return out.reshape(fields.shape)


def solution(mesh):
    placed = (P(None, None, "gz", "gx"), P("gz"))
    return jax.shard_map(
        body, mesh=mesh, in_specs=placed, out_specs=P(None, None, "gz", "gx"), check_vma=False
    )
```
